256 devices in a mesh: ctx: 32 (over x, y, z_hi), grp: 8 (over z_lo, core).
Axes of the slice: x: 4, y: 4, z: 8 (z_hi: 2, z_lo: 4; z = z_hi * 4 + z_lo), core: 2. Of those that a mesh axis runs over, the one named last changes fastest.
Arguments:
- tokens: bfloat16 [16384, 4096], P('ctx'), may hold values from -6 to 6
- w_z: bfloat16 [4096, 8192], P('ctx', 'grp'), may hold values from -0.09375 to 0.09375
- w_x: bfloat16 [4096, 8192], P('ctx', 'grp'), may hold values from -0.09375 to 0.09375
- w_bc: bfloat16 [4096, 8, 256], P('ctx', 'grp'), may hold values from -0.09375 to 0.09375
- w_dt: bfloat16 [4096, 128], P('ctx', 'grp'), may hold values from -0.09375 to 0.09375
- conv_x: float32 [4, 8192], P(None, 'grp'), may hold values from -3 to 3
- conv_bc: float32 [4, 8, 256], P(None, 'grp'), may hold values from -3 to 3
- bias_x: float32 [8192], P('grp'), may hold values from -3 to 3
- bias_bc: float32 [8, 256], P('grp'), may hold values from -3 to 3
- dt_bias: float32 [128], P('grp'), may hold values from -5.3 to -3
- a_log: float32 [128], P('grp'), as said below
- d_skip: float32 [128], P('grp'), may hold values from 0.5 to 1.5
- norm_gain: float32 [8192], P('grp'), may hold values from 0.5 to 1.5
Outputs:
- layer_out: bfloat16 [16384, 8192], P('ctx', 'grp')
The draws below stay inside these ranges and needn't reach their ends.
Inputs may be any that keep to these rules, and one draw needn't show every extreme that they name: `a_log`: each head's log decay rate; some heads forget within tens of tokens, others keep much of their state over all 16384 tokens.
All inputs are finite; a program needn't handle non-finite values.
Results may differ from the reference program's by a relative error of at most 0.013.
Values may be sent and summed in bfloat16 or wider, within the bound.
No kernel may reach another device: no remote copies, remote signals or barrier semaphores. Data moves between devices by JAX's collectives and lax.ppermute only.
A program may use at most 128 MiB of HBM per device.

```python
import math
import jax
import jax.numpy as jnp
from jax import lax

D = 4096
HEADS = 128
HEAD_DIM = 64
STATE = 128
GROUPS = 8
CONV = 4
SPAN = 256
TOKENS = 16384


def draw_a_log(key, part):
    key_pick, key_fast, key_slow = jax.random.split(jax.random.fold_in(key, 11), 3)
    fast_share = 0.5
    picked = jax.random.uniform(key_pick, (HEADS,), jnp.float32) < fast_share
    fast_log = jax.random.uniform(key_fast, (HEADS,), jnp.float32, 0.0, 3.0)
    slow_log = jax.random.uniform(key_slow, (HEADS,), jnp.float32, math.log(0.3), math.log(2.0)) - math.log(0.02 * TOKENS)
    return jnp.where(picked, fast_log, slow_log).astype(jnp.float32)


def steps_of(key, extent, cuts, low, top_value):
    factor_of, own = 1.0, jax.random.fold_in(key, 6)
    for position, shards_of in cuts:
        heights = jnp.exp(jax.random.uniform(jax.random.fold_in(own, position), (shards_of,), jnp.float32, low / len(cuts), top_value / len(cuts)))
        factor_of = factor_of * jnp.repeat(heights, extent[position] // shards_of).reshape([-1 if axis == position else 1 for axis in range(len(extent))])
    return factor_of


def bell_draw(own_key, extent, width, bound, cuts=(), dtype=jnp.bfloat16):
    values = width * jax.random.normal(own_key, extent, jnp.float32)
    if cuts:
        values = values * steps_of(own_key, extent, cuts, -0.22, 0.18)
    return jnp.clip(values, -bound, bound).astype(dtype)


def setup_inputs(seed: int = 0) -> dict:
    keys = jax.random.split(jax.random.key(seed), 14)
    return {
        "tokens": bell_draw(keys[0], (TOKENS, D), 1.0, 6.0, ((0, 32),)),
        "w_z": bell_draw(keys[1], (D, HEADS * HEAD_DIM), D ** -0.5, 0.09375, ((0, 32), (1, 8))),
        "w_x": bell_draw(keys[2], (D, HEADS * HEAD_DIM), D ** -0.5, 0.09375, ((0, 32), (1, 8))),
        "w_bc": bell_draw(keys[3], (D, GROUPS, 2 * STATE), D ** -0.5, 0.09375, ((0, 32), (1, 8))),
        "w_dt": bell_draw(keys[4], (D, HEADS), D ** -0.5, 0.09375, ((0, 32), (1, 8))),
        "conv_x": bell_draw(keys[5], (CONV, HEADS * HEAD_DIM), CONV ** -0.5, 3.0, ((1, 8),), jnp.float32),
        "conv_bc": bell_draw(keys[6], (CONV, GROUPS, 2 * STATE), CONV ** -0.5, 3.0, ((1, 8),), jnp.float32),
        "bias_x": bell_draw(keys[7], (HEADS * HEAD_DIM,), 0.5, 3.0, ((0, 8),), jnp.float32),
        "bias_bc": bell_draw(keys[8], (GROUPS, 2 * STATE), 0.5, 3.0, ((0, 8),), jnp.float32),
        "dt_bias": jnp.clip(-5.3 + 2.3000002 * jax.random.uniform(keys[9], (HEADS,), jnp.float32) ** steps_of(keys[9], (HEADS,), ((0, 8),), -0.2, 0.2), -5.3, -3.0),
        "a_log": draw_a_log(jax.random.fold_in(keys[13], 71), 0),
        "d_skip": jnp.clip(0.5 + 1.0 * jax.random.uniform(keys[11], (HEADS,), jnp.float32) ** steps_of(keys[11], (HEADS,), ((0, 8),), -0.2, 0.2), 0.5, 1.5),
        "norm_gain": jnp.clip(1.0 + 0.1 * jax.random.normal(keys[12], (HEADS * HEAD_DIM,), jnp.float32), 0.5, 1.5),
    }


def causal_taps(extended, taps, offset_bias):
    running = jnp.zeros((SPAN, taps.shape[1]), jnp.float32) + offset_bias[None, :]
    for tap in range(CONV):
        running = running + taps[tap][None, :] * extended[tap:tap + SPAN].astype(jnp.float32)
    return jax.nn.silu(running).astype(jnp.bfloat16)

def reference(tokens, w_z, w_x, w_bc, w_dt, conv_x, conv_bc, bias_x, bias_bc, dt_bias, a_log, d_skip, norm_gain):
    per_group = HEADS // GROUPS
    bc_width = GROUPS * 2 * STATE
    inner_width = HEADS * HEAD_DIM
    w_mix = w_bc.reshape(D, bc_width)
    conv_mix = conv_bc.reshape(CONV, bc_width)
    bias_mix = bias_bc.reshape(bc_width)
    decay_rate = jnp.exp(a_log)
    causal_mask = jnp.arange(SPAN)[:, None] >= jnp.arange(SPAN)[None, :]

    def advance(carry, block_tokens):
        state, prev_inner, prev_mix = carry
        gate_rows = jnp.dot(block_tokens, w_z, preferred_element_type=jnp.float32).astype(jnp.bfloat16)
        inner = jnp.dot(block_tokens, w_x, preferred_element_type=jnp.float32).astype(jnp.bfloat16)
        mixed = jnp.dot(block_tokens, w_mix, preferred_element_type=jnp.float32).astype(jnp.bfloat16)
        step_raw = jnp.dot(block_tokens, w_dt, preferred_element_type=jnp.float32)
        inner_c = causal_taps(jnp.concatenate([prev_inner, inner], axis=0), conv_x, bias_x)
        mix_c = causal_taps(jnp.concatenate([prev_mix, mixed], axis=0), conv_mix, bias_mix)
        mix_c = mix_c.reshape(SPAN, GROUPS, 2 * STATE)
        b_in = mix_c[:, :, :STATE].astype(jnp.float32)
        c_in = mix_c[:, :, STATE:].astype(jnp.float32)
        step_size = jax.nn.softplus(step_raw + dt_bias[None, :])
        cumul = jnp.cumsum(-decay_rate[None, :] * step_size, axis=0)
        scores = jnp.einsum('ign,jgn->gij', c_in, b_in)
        scores_h = jnp.repeat(scores, per_group, axis=0)
        cumul_t = cumul.T
        log_gap = cumul_t[:, :, None] - cumul_t[:, None, :]
        decay_mat = jnp.where(causal_mask[None], jnp.exp(jnp.minimum(log_gap, 0.0)), 0.0)
        weight = (scores_h * decay_mat * step_size.T[:, None, :]).astype(jnp.bfloat16)
        inner_h = inner_c.reshape(SPAN, HEADS, HEAD_DIM).astype(jnp.float32)
        intra = jnp.einsum('hij,jhp->ihp', weight.astype(jnp.float32), inner_h)
        c_heads = jnp.repeat(c_in, per_group, axis=1)
        inter = jnp.einsum('ihn,hnp->ihp', c_heads, state, precision=lax.Precision.HIGHEST) * jnp.exp(cumul)[:, :, None]
        scan_out = intra + inter + d_skip[None, :, None] * inner_h
        block_log = cumul[-1]
        b_heads = jnp.repeat(b_in, per_group, axis=1)
        weighted_b = ((jnp.exp(block_log[None, :] - cumul) * step_size)[:, :, None] * b_heads).astype(jnp.bfloat16)
        local_state = jnp.einsum('jhn,jhp->hnp', weighted_b.astype(jnp.float32), inner_h)
        new_state = jnp.exp(block_log)[:, None, None] * state + local_state
        gated = scan_out.reshape(SPAN, inner_width) * jax.nn.silu(gate_rows.astype(jnp.float32))
        grouped = gated.reshape(SPAN, GROUPS, per_group * HEAD_DIM)
        scale = lax.rsqrt(lax.optimization_barrier(jnp.mean(grouped * grouped, axis=-1, keepdims=True)) + 1e-05)
        result = ((grouped * scale).reshape(SPAN, inner_width) * norm_gain[None, :]).astype(jnp.bfloat16)
        return ((new_state, inner[SPAN - (CONV - 1):], mixed[SPAN - (CONV - 1):]), result)
    init = (jnp.zeros((HEADS, STATE, HEAD_DIM), jnp.float32), jnp.zeros((CONV - 1, inner_width), jnp.bfloat16), jnp.zeros((CONV - 1, bc_width), jnp.bfloat16))
    blocks = tokens.reshape(TOKENS // SPAN, SPAN, D)
    final_carry, results = lax.scan(advance, init, blocks)
    return results.reshape(TOKENS, inner_width)
```

```python
import jax
import jax.numpy as jnp
from jax import lax
from jax.experimental import pallas as pl
from jax.experimental.pallas import tpu as pltpu
from jax.sharding import PartitionSpec as P

SPAN = 256
EDGE = 16
LIMIT = 20
HOPS = (8, 24, 2, 6)
ZHOP = 1


def swap(value, mask):
    count = lax.axis_size("ctx")
    return lax.ppermute(value, "ctx", [(i, i ^ mask) for i in range(count)])


def order(q):
    return [HOPS[(q + k) % 4] for k in range(4)]


def masks(q, zs):
    out = []
    for s in range(16):
        m = 0
        for k in range(4):
            if s >> k & 1:
                m ^= order(q)[k]
        out.extend(m ^ z for z in zs)
    return out


def hop(value, mask, scope):
    with jax.named_scope(scope):
        return swap(value, mask)


def gather(pieces, scope):
    now = list(pieces)
    got = first = None
    for k in range(4):
        got = [hop(now[q], order(q)[k], f"{scope}_hop{k}_part{q}") for q in range(4)]
        if k < 3:
            now = [jnp.concatenate([now[q], got[q]], axis=0) for q in range(4)]
        if k == 0:
            first = now
    return now, got, first


def after(value, *others):
    return lax.optimization_barrier((value,) + others)[0]


def columns_of(tok_ref, idx_ref, wanted):
    return jnp.concatenate(
        [tok_ref[:, pl.ds(pl.multiple_of(idx_ref[m] * 128, 128), 128)] for m in wanted], axis=1
    )


def side(tok_ref, idx_ref, w, wanted):
    count = len(wanted)
    lhs = columns_of(tok_ref, idx_ref, wanted)
    rhs = w[:, 0:128, :].reshape(count * 128, w.shape[2])
    return jnp.dot(lhs, rhs, preferred_element_type=jnp.float32)


def mixed(tok_ref, idx_ref, early, late, slots):
    ms = sorted(slots[0])
    lhs = columns_of(tok_ref, idx_ref, ms)
    parts = []
    for m in ms:
        for q in range(4):
            s = slots[q][m]
            w = early[q] if s < 16 else late[q]
            parts.append(w[s % 16, 128:160, :])
    rhs = jnp.concatenate(parts, axis=0)
    return jnp.dot(lhs, rhs, preferred_element_type=jnp.float32)


VM = pl.BlockSpec(memory_space=pltpu.VMEM)
SM = pl.BlockSpec(memory_space=pltpu.SMEM)


def call(kernel, shapes, n_in, smem=1, limit=LIMIT, name=None, scratch=(), cost=None):
    return pl.pallas_call(
        kernel,
        out_shape=shapes,
        in_specs=[SM] * smem + [VM] * (n_in - smem),
        out_specs=jax.tree.map(lambda _: VM, shapes),
        scratch_shapes=scratch,
        cost_estimate=cost and pl.CostEstimate(flops=cost, transcendentals=0, bytes_accessed=0),
        compiler_params=pltpu.CompilerParams(vmem_limit_bytes=limit << 20),
        name=name,
    )


def scan_kernel(
    p_ref, cum_c, cum_r, taps_x, taps_b, bias_x, bias_b, skip, end_c, logs,
    y_ref, c_ref, s_ref, xs, bs,
):
    xs[...] = p_ref[:, 0:1024].astype(jnp.float32)
    bs[...] = p_ref[:, 1024:1280].astype(jnp.float32)
    ii = lax.broadcasted_iota(jnp.int32, (SPAN, SPAN), 0)
    jj = lax.broadcasted_iota(jnp.int32, (SPAN, SPAN), 1)
    mask = ii >= jj
    heads = cum_c.shape[1]
    for b in range(2):
        base = EDGE + b * SPAN - 3

        def conv(ref, taps, bias):
            run = jnp.broadcast_to(bias[...], (SPAN, ref.shape[1]))
            for tap in range(4):
                run = run + taps[tap : tap + 1, :] * ref[base + tap : base + tap + SPAN, :]
            return run / (1.0 + jnp.exp(-run))

        x_c = conv(xs, taps_x, bias_x).astype(jnp.bfloat16)
        bc = conv(bs, taps_b, bias_b).astype(jnp.bfloat16)
        b_in, c_in = bc[:, 0:128], bc[:, 128:256]
        rows = slice(b * SPAN, b * SPAN + SPAN)
        c_ref[rows, :] = c_in
        scores = lax.dot_general(
            c_in, b_in, (((1,), (1,)), ((), ())), preferred_element_type=jnp.float32
        )
        x_f = x_c.astype(jnp.float32)
        before = None
        if b == 1:
            before = jnp.dot(
                c_in, s_ref[0:128, :].astype(jnp.bfloat16), preferred_element_type=jnp.float32
            )
        scaled = []
        for h in range(heads):
            lanes = slice(64 * h, 64 * h + 64)
            col = cum_c[rows, h : h + 1]
            gap = jnp.where(mask, col - cum_r[h : h + 1, rows], -1e30)
            weight = (jnp.exp(gap) * scores).astype(jnp.bfloat16)
            y = jnp.dot(weight, x_c[:, lanes], preferred_element_type=jnp.float32)
            y = y + skip[0:1, lanes] * x_f[:, lanes]
            if b == 1:
                y = y + jnp.exp(col) * before[:, lanes]
            y_ref[rows, lanes] = y
            scaled.append((end_c[rows, h : h + 1] * x_f[:, lanes]).astype(jnp.bfloat16))
        xw = jnp.concatenate(scaled, axis=1)
        state = lax.dot_general(
            b_in, xw, (((0,), (0,)), ((), ())), preferred_element_type=jnp.float32
        )
        if b == 0:
            s_ref[...] = state
        else:
            s_ref[...] = jnp.exp(logs[1:2, :]) * s_ref[...] + state


def step_kernel(idx_ref, tok_ref, near, far, bias, a_log, cum_c, cum_r, end_c, grow, logs):
    rows, heads = cum_c.shape
    raw = jnp.zeros((rows, heads), jnp.float32)
    order_of = masks(0, (0, 1))
    for half, ref in enumerate((near, far)):
        lhs = columns_of(tok_ref, idx_ref, order_of[16 * half : 16 * half + 16])
        parts = []
        for s in range(16):
            w = ref[s].astype(jnp.float32)
            parts.append(jnp.concatenate([w[:, 0:128], w[:, 128:256]], axis=0))
        rhs = jnp.concatenate(parts, axis=1).astype(jnp.bfloat16)
        raw = raw + lax.dot_general(
            lhs, rhs, (((1,), (1,)), ((), ())), preferred_element_type=jnp.float32
        )
    raw = raw + bias[...]
    step = jnp.maximum(raw, 0.0) + jnp.log1p(jnp.exp(-jnp.abs(raw)))
    rate = -jnp.exp(a_log[...]) * step
    ii = lax.broadcasted_iota(jnp.int32, (SPAN, SPAN), 0)
    jj = lax.broadcasted_iota(jnp.int32, (SPAN, SPAN), 1)
    tri = jnp.where(ii >= jj, 1.0, 0.0)
    start = jnp.zeros((1, heads), jnp.float32)
    for b in range(rows // SPAN):
        span = slice(b * SPAN, b * SPAN + SPAN)
        cum = jnp.dot(
            tri, rate[span], preferred_element_type=jnp.float32, precision=lax.Precision.HIGHEST
        )
        last = cum[SPAN - 1 : SPAN, :]
        cum_c[span, :] = cum
        end_c[span, :] = jnp.exp(last - cum) * step[span]
        grow[span, :] = jnp.exp(cum + start)
        start = start + last
        side_by = cum - jnp.log(step[span])
        wide = jnp.concatenate([side_by, jnp.zeros((SPAN, 128 - heads), jnp.float32)], axis=1)
        cum_r[:, span] = wide.T[0:heads, :]
    for h in range(heads):
        lanes = slice(64 * h, 64 * h + 64)
        logs[0:1, lanes] = jnp.broadcast_to(start[:, h : h + 1], (1, 64))
        logs[1:2, lanes] = jnp.broadcast_to(last[:, h : h + 1], (1, 64))


def gate_kernel(idx_ref, tok_ref, *refs):
    for q in range(4):
        lanes = slice(256 * q, 256 * q + 256)
        refs[4][:, lanes] = side(tok_ref, idx_ref, refs[q], masks(q, (0, 1))[0:16])


def final_kernel(
    idx_ref, tok_ref, w0, w1, w2, w3, za, y_ref, c_ref, s_ref, grow, gain, out_ref, gate
):
    for q, w in enumerate((w0, w1, w2, w3)):
        lanes = slice(256 * q, 256 * q + 256)
        gate[:, lanes] = za[:, lanes] + side(tok_ref, idx_ref, w, masks(q, (0, 1))[16:32])
    inter = jnp.dot(c_ref[...], s_ref[...], preferred_element_type=jnp.float32)
    heads = grow.shape[1]
    total = jnp.zeros((out_ref.shape[0], 1), jnp.float32)
    kept = []
    for h in range(heads // 2):
        lanes = slice(128 * h, 128 * h + 128)
        low = jnp.broadcast_to(grow[:, 2 * h : 2 * h + 1], (out_ref.shape[0], 128))
        high = jnp.broadcast_to(grow[:, 2 * h + 1 : 2 * h + 2], (out_ref.shape[0], 128))
        lane = lax.broadcasted_iota(jnp.int32, (1, 128), 1)
        v = y_ref[:, lanes] + jnp.where(lane < 64, low, high) * inter[:, lanes]
        g = gate[:, lanes].astype(jnp.bfloat16).astype(jnp.float32)
        v = v * (g / (1.0 + jnp.exp(-g)))
        total = total + jnp.sum(v * v, axis=1, keepdims=True)
        kept.append(v)
    scale = lax.rsqrt(total / out_ref.shape[1] + 1e-05)
    for h in range(heads // 2):
        lanes = slice(128 * h, 128 * h + 128)
        out_ref[:, lanes] = (kept[h] * scale * gain[0:1, lanes]).astype(jnp.bfloat16)


def split(value):
    high = lax.reduce_precision(value, 8, 7)
    return high.astype(jnp.bfloat16), (value - high).astype(jnp.bfloat16)


def pack(state, log):
    high, low = split(log)
    tail = jnp.zeros((6,) + log.shape, jnp.bfloat16)
    return jnp.concatenate([state.astype(jnp.bfloat16), high[None], low[None], tail], axis=0)


def unpack(message):
    message = message.astype(jnp.float32)
    return message[0:128], message[128] + message[129]


def on_device(
    tokens, w_z, w_x, w_bc, w_dt, conv_x, conv_bc, bias_x, bias_bc, dt_bias, a_log, d_skip, norm_gain
):
    f32, bf16 = jnp.float32, jnp.bfloat16
    rows = tokens.shape[0]
    heads = w_dt.shape[1]
    me = lax.axis_index("ctx")
    count = lax.axis_size("ctx")
    idx = me.astype(jnp.int32) ^ jnp.arange(count, dtype=jnp.int32)
    wide = rows + EDGE
    low = me % 2 == 0

    turned = w_dt.T
    turned = jnp.concatenate([turned[0:8], turned[8:16]], axis=1)
    mix_dt = jnp.concatenate([w_bc.reshape(128, 256), turned], axis=0)
    far_x = hop(w_x, ZHOP, "far_x_rows")
    far_mix = hop(mix_dt, ZHOP, "far_mix_rows")
    edge = lax.ppermute(tokens[rows - EDGE :], "ctx", [(i, i + 1) for i in range(count - 1)])
    far_z = hop(w_z, ZHOP, "far_gate_rows")
    tok = jnp.concatenate([edge, tokens], axis=0)

    def part_of(wide_part, mix_part, q):
        piece = [wide_part[:, 256 * q : 256 * q + 256], mix_part[32 * q : 32 * q + 32]]
        if q == 0:
            piece.append(mix_part[128:136])
        return jnp.concatenate(piece, axis=0)

    both_x = [jnp.stack([part_of(w_x, mix_dt, q), part_of(far_x, far_mix, q)]) for q in range(4)]
    x_early, x_late, _ = gather(both_x, "value")
    both_z = [
        jnp.stack([w_z[:, 256 * q : 256 * q + 256], far_z[:, 256 * q : 256 * q + 256]])
        for q in range(4)
    ]
    z_early, z_late, z_first = gather([after(both_z[q], x_late[max(q, 1)]) for q in range(4)], "gate")
    slots = [{m: s for s, m in enumerate(masks(q, (0, 1)))} for q in range(4)]

    cumul, cum_r, end_c, grow, logs = call(
        step_kernel,
        (
            jax.ShapeDtypeStruct((rows, heads), f32),
            jax.ShapeDtypeStruct((heads, rows), f32),
            jax.ShapeDtypeStruct((rows, heads), f32),
            jax.ShapeDtypeStruct((rows, heads), f32),
            jax.ShapeDtypeStruct((2, 1024), f32),
        ),
        6,
        name="steps",
    )(idx, tokens, x_early[0][:, 160:168], x_late[0][:, 160:168], dt_bias[None], a_log[None])

    def early_kernel(idx_ref, tok_ref, *refs):
        for q in range(4):
            refs[4][:, 256 * q : 256 * q + 256] = side(
                tok_ref, idx_ref, refs[q], masks(q, (0, 1))[0:16]
            )

    def late_kernel(idx_ref, tok_ref, part_ref, *refs):
        early, late, out_ref = refs[0:4], refs[4:8], refs[8]
        for q in range(4):
            lanes = slice(256 * q, 256 * q + 256)
            part = side(tok_ref, idx_ref, late[q], masks(q, (0, 1))[16:32])
            out_ref[:, lanes] = (part + part_ref[:, lanes]).astype(bf16)
        part = mixed(tok_ref, idx_ref, early, late, slots)
        out_ref[:, 1024:1280] = part.astype(bf16)

    part = call(early_kernel, jax.ShapeDtypeStruct((wide, 1024), f32), 6, name="early_x")(
        idx, tok, *x_early
    )
    inner = call(late_kernel, jax.ShapeDtypeStruct((wide, 1280), bf16), 11, name="late_x")(
        idx, tok, part, *x_early, *x_late
    )

    skip = jnp.repeat(d_skip, 64)[None]
    y, c_in, state = call(
        scan_kernel,
        (
            jax.ShapeDtypeStruct((rows, 1024), f32),
            jax.ShapeDtypeStruct((rows, 128), bf16),
            jax.ShapeDtypeStruct((128, 1024), f32),
        ),
        10,
        smem=0,
        name="scan",
        scratch=(pltpu.VMEM((wide, 1024), f32), pltpu.VMEM((wide, 256), f32)),
    )(
        after(inner, *z_first), cumul, cum_r, conv_x, conv_bc.reshape(4, 256), bias_x[None],
        bias_bc.reshape(1, 256), skip, end_c, logs,
    )
    za = call(gate_kernel, jax.ShapeDtypeStruct((rows, 1024), f32), 6, name="gate")(
        idx, tokens, *z_early
    )

    total = logs[0]

    def halves(value):
        left, right = value[..., 0:512], value[..., 512:1024]
        return jnp.where(low, left, right), jnp.where(low, right, left)

    mine, other = halves(state)
    my_log, other_log = halves(total)
    come, come_log = unpack(swap(pack(other, other_log), ZHOP))
    first, last = jnp.where(low, mine, come), jnp.where(low, come, mine)
    first_log, last_log = jnp.where(low, my_log, come_log), jnp.where(low, come_log, my_log)
    whole = jnp.exp(last_log)[None] * first + last
    whole_log = first_log + last_log
    before = jnp.zeros_like(whole)
    lead = jnp.zeros_like(whole_log)
    place = me // 2
    for mask, width in ((1, 1), (3, 2), (4, 4), (12, 8)):
        got, got_log = unpack(swap(pack(whole, whole_log), mask * 2))
        earlier = (place ^ mask) // width < place // width
        before = before + jnp.where(earlier, jnp.exp(lead), 0.0)[None] * got
        whole = (
            jnp.where(earlier, 1.0, jnp.exp(got_log))[None] * whole
            + jnp.where(earlier, jnp.exp(whole_log), 1.0)[None] * got
        )
        lead = lead + jnp.where(earlier, got_log, 0.0)
        whole_log = whole_log + got_log
    beyond = jnp.exp(first_log)[None] * before + first
    keep = jnp.where(low, before, beyond).astype(bf16)
    come = swap(jnp.where(low, beyond, before).astype(bf16), ZHOP)
    carried = jnp.concatenate([jnp.where(low, keep, come), jnp.where(low, come, keep)], axis=1)

    return call(
        final_kernel,
        jax.ShapeDtypeStruct((rows, 1024), bf16),
        12,
        name="final",
        scratch=(pltpu.VMEM((rows, 1024), f32),),
    )(idx, tokens, *z_late, za, y, c_in, carried, grow, norm_gain[None])


def solution(mesh):
    placed = (
        P("ctx", None),
        P("ctx", "grp"),
        P("ctx", "grp"),
        P("ctx", "grp", None),
        P("ctx", "grp"),
        P(None, "grp"),
        P(None, "grp", None),
        P("grp"),
        P("grp", None),
        P("grp"),
        P("grp"),
        P("grp"),
        P("grp"),
    )
    return jax.shard_map(
        on_device, mesh=mesh, in_specs=placed, out_specs=P("ctx", "grp"), check_vma=False
    )
```

```python
import jax
import jax.numpy as jnp
from jax import lax
from jax.experimental import pallas as pl
from jax.experimental.pallas import tpu as pltpu
from jax.sharding import PartitionSpec as P

SPAN = 256
EDGE = 16
LIMIT = 12
HOPS = (8, 24, 2, 6)
ZHOP = 1


def swap(value, mask):
    count = lax.axis_size("ctx")
    return lax.ppermute(value, "ctx", [(i, i ^ mask) for i in range(count)])


def order(q):
    return [HOPS[(q + k) % 4] for k in range(4)]


def masks(q, zs):
    out = []
    for s in range(16):
        m = 0
        for k in range(4):
            if s >> k & 1:
                m ^= order(q)[k]
        out.extend(m ^ z for z in zs)
    return out


def hop(value, mask, scope):
    with jax.named_scope(scope):
        return swap(value, mask)


def gather_some(pieces, scope):
    now = list(pieces)
    for k in range(3):
        got = [hop(now[q], order(q)[k], f"{scope}_hop{k}_part{q}") for q in range(4)]
        now = [jnp.concatenate([now[q], got[q]], axis=0) for q in range(4)]
    return now


def gather_rest(now, scope):
    return [hop(now[q], order(q)[3], f"{scope}_hop3_part{q}") for q in range(4)]


def after(value, *others):
    return lax.optimization_barrier((value,) + others)[0]


def columns_of(tok_ref, idx_ref, wanted):
    return jnp.concatenate(
        [tok_ref[:, pl.ds(pl.multiple_of(idx_ref[m] * 128, 128), 128)] for m in wanted], axis=1
    )


def side(tok_ref, idx_ref, w, wanted):
    count = len(wanted)
    lhs = columns_of(tok_ref, idx_ref, wanted)
    rhs = w[:, 0:128, :].reshape(count * 128, w.shape[2])
    return jnp.dot(lhs, rhs, preferred_element_type=jnp.float32)


def mixed(tok_ref, idx_ref, early, late, slots):
    ms = sorted(slots[0])
    lhs = columns_of(tok_ref, idx_ref, ms)
    parts = []
    for m in ms:
        for q in range(4):
            s = slots[q][m]
            w = early[q] if s < 16 else late[q]
            parts.append(w[s % 16, 128:160, :])
    rhs = jnp.concatenate(parts, axis=0)
    return jnp.dot(lhs, rhs, preferred_element_type=jnp.float32)


VM = pl.BlockSpec(memory_space=pltpu.VMEM)
SM = pl.BlockSpec(memory_space=pltpu.SMEM)


def call(kernel, shapes, n_in, smem=1, limit=LIMIT, name=None, scratch=(), cost=None):
    return pl.pallas_call(
        kernel,
        out_shape=shapes,
        in_specs=[SM] * smem + [VM] * (n_in - smem),
        out_specs=jax.tree.map(lambda _: VM, shapes),
        scratch_shapes=scratch,
        cost_estimate=cost and pl.CostEstimate(flops=cost, transcendentals=0, bytes_accessed=0),
        compiler_params=pltpu.CompilerParams(vmem_limit_bytes=limit << 20),
        name=name,
    )


def state_kernel(p_ref, taps_x, taps_b, bias_x, bias_b, end_c, logs, x_ref, bc_ref, s_ref, mid_ref, xs, bs):
    xs[...] = p_ref[:, 0:1024].astype(jnp.float32)
    bs[...] = p_ref[:, 1024:1280].astype(jnp.float32)
    for b in range(2):
        base = EDGE + b * SPAN - 3

        def conv(ref, taps, bias):
            run = jnp.broadcast_to(bias[...], (SPAN, ref.shape[1]))
            for tap in range(4):
                run = run + taps[tap : tap + 1, :] * ref[base + tap : base + tap + SPAN, :]
            return run / (1.0 + jnp.exp(-run))

        x_c = conv(xs, taps_x, bias_x).astype(jnp.bfloat16)
        bc = conv(bs, taps_b, bias_b).astype(jnp.bfloat16)
        rows = slice(b * SPAN, b * SPAN + SPAN)
        x_ref[rows, :] = x_c
        bc_ref[rows, :] = bc
        x_f = x_c.astype(jnp.float32)
        scaled = []
        for h in range(end_c.shape[1]):
            lanes = slice(64 * h, 64 * h + 64)
            scaled.append((end_c[rows, h : h + 1] * x_f[:, lanes]).astype(jnp.bfloat16))
        xw = jnp.concatenate(scaled, axis=1)
        state = lax.dot_general(
            bc[:, 0:128], xw, (((0,), (0,)), ((), ())), preferred_element_type=jnp.float32
        )
        if b == 0:
            s_ref[...] = state
            mid_ref[...] = state.astype(jnp.bfloat16)
        else:
            s_ref[...] = jnp.exp(logs[1:2, :]) * s_ref[...] + state


def scan_kernel(b, x_ref, bc_ref, mid_ref, cum_c, cum_r, skip, y_ref):
    ii = lax.broadcasted_iota(jnp.int32, (SPAN, SPAN), 0)
    jj = lax.broadcasted_iota(jnp.int32, (SPAN, SPAN), 1)
    mask = ii >= jj
    rows = slice(b * SPAN, b * SPAN + SPAN)
    b_in, c_in = bc_ref[rows, 0:128], bc_ref[rows, 128:256]
    scores = lax.dot_general(
        c_in, b_in, (((1,), (1,)), ((), ())), preferred_element_type=jnp.float32
    )
    before = None
    if b == 1:
        before = jnp.dot(c_in, mid_ref[...], preferred_element_type=jnp.float32)
    for h in range(cum_c.shape[1]):
        lanes = slice(64 * h, 64 * h + 64)
        col = cum_c[rows, h : h + 1]
        gap = jnp.where(mask, col - cum_r[h : h + 1, rows], -1e30)
        weight = (jnp.exp(gap) * scores).astype(jnp.bfloat16)
        x_h = x_ref[rows, lanes]
        y = jnp.dot(weight, x_h, preferred_element_type=jnp.float32)
        y = y + skip[0:1, lanes] * x_h.astype(jnp.float32)
        if b == 1:
            y = y + jnp.exp(col) * before[:, lanes]
        y_ref[:, lanes] = y


def step_kernel(idx_ref, tok_ref, near, far, bias, a_log, cum_c, cum_r, end_c, grow, logs):
    rows, heads = cum_c.shape
    raw = jnp.zeros((rows, heads), jnp.float32)
    order_of = masks(1, (0, 1))
    for half, ref in enumerate((near, far)):
        lhs = columns_of(tok_ref, idx_ref, order_of[16 * half : 16 * half + 16])
        parts = []
        for s in range(16):
            w = ref[s].astype(jnp.float32)
            parts.append(jnp.concatenate([w[:, 0:128], w[:, 128:256]], axis=0))
        rhs = jnp.concatenate(parts, axis=1).astype(jnp.bfloat16)
        raw = raw + lax.dot_general(
            lhs, rhs, (((1,), (1,)), ((), ())), preferred_element_type=jnp.float32
        )
    raw = raw + bias[...]
    step = jnp.maximum(raw, 0.0) + jnp.log1p(jnp.exp(-jnp.abs(raw)))
    rate = -jnp.exp(a_log[...]) * step
    ii = lax.broadcasted_iota(jnp.int32, (SPAN, SPAN), 0)
    jj = lax.broadcasted_iota(jnp.int32, (SPAN, SPAN), 1)
    tri = jnp.where(ii >= jj, 1.0, 0.0)
    start = jnp.zeros((1, heads), jnp.float32)
    for b in range(rows // SPAN):
        span = slice(b * SPAN, b * SPAN + SPAN)
        cum = jnp.dot(
            tri, rate[span], preferred_element_type=jnp.float32, precision=lax.Precision.HIGHEST
        )
        last = cum[SPAN - 1 : SPAN, :]
        cum_c[span, :] = cum
        end_c[span, :] = jnp.exp(last - cum) * step[span]
        grow[span, :] = jnp.exp(cum + start)
        start = start + last
        side_by = cum - jnp.log(step[span])
        wide = jnp.concatenate([side_by, jnp.zeros((SPAN, 128 - heads), jnp.float32)], axis=1)
        cum_r[:, span] = wide.T[0:heads, :]
    for h in range(heads):
        lanes = slice(64 * h, 64 * h + 64)
        logs[0:1, lanes] = jnp.broadcast_to(start[:, h : h + 1], (1, 64))
        logs[1:2, lanes] = jnp.broadcast_to(last[:, h : h + 1], (1, 64))


def gate_kernel(idx_ref, tok_ref, *refs):
    for q in range(4):
        lanes = slice(256 * q, 256 * q + 256)
        refs[4][:, lanes] = side(tok_ref, idx_ref, refs[q], masks(q, (0, 1))[0:16])


def gate_late_kernel(idx_ref, tok_ref, w0, w1, w2, w3, za, out_ref):
    for q, w in enumerate((w0, w1, w2, w3)):
        lanes = slice(256 * q, 256 * q + 256)
        g = za[:, lanes] + side(tok_ref, idx_ref, w, masks(q, (0, 1))[16:32])
        g = g.astype(jnp.bfloat16).astype(jnp.float32)
        out_ref[:, lanes] = g / (1.0 + jnp.exp(-g))


def final_kernel(gate, y0, y1, c_ref, s_ref, grow, gain, out_ref):
    inter = jnp.dot(c_ref[:, 128:256], s_ref[...], preferred_element_type=jnp.float32)
    heads = grow.shape[1]
    total = jnp.zeros((out_ref.shape[0], 1), jnp.float32)
    kept = []
    for h in range(heads // 2):
        lanes = slice(128 * h, 128 * h + 128)
        low = jnp.broadcast_to(grow[:, 2 * h : 2 * h + 1], (out_ref.shape[0], 128))
        high = jnp.broadcast_to(grow[:, 2 * h + 1 : 2 * h + 2], (out_ref.shape[0], 128))
        lane = lax.broadcasted_iota(jnp.int32, (1, 128), 1)
        y = jnp.concatenate([y0[:, lanes], y1[:, lanes]], axis=0)
        v = y + jnp.where(lane < 64, low, high) * inter[:, lanes]
        v = v * gate[:, lanes]
        total = total + jnp.sum(v * v, axis=1, keepdims=True)
        kept.append(v)
    scale = lax.rsqrt(total / out_ref.shape[1] + 1e-05)
    for h in range(heads // 2):
        lanes = slice(128 * h, 128 * h + 128)
        out_ref[:, lanes] = (kept[h] * scale * gain[0:1, lanes]).astype(jnp.bfloat16)


def split(value):
    high = lax.reduce_precision(value, 8, 7)
    return high.astype(jnp.bfloat16), (value - high).astype(jnp.bfloat16)


def pack(state, log):
    high, low = split(log)
    tail = jnp.zeros((6,) + log.shape, jnp.bfloat16)
    return jnp.concatenate([state.astype(jnp.bfloat16), high[None], low[None], tail], axis=0)


def unpack(message):
    message = message.astype(jnp.float32)
    return message[0:128], message[128] + message[129]


def on_device(
    tokens, w_z, w_x, w_bc, w_dt, conv_x, conv_bc, bias_x, bias_bc, dt_bias, a_log, d_skip, norm_gain
):
    f32, bf16 = jnp.float32, jnp.bfloat16
    rows = tokens.shape[0]
    heads = w_dt.shape[1]
    me = lax.axis_index("ctx")
    count = lax.axis_size("ctx")
    idx = me.astype(jnp.int32) ^ jnp.arange(count, dtype=jnp.int32)
    wide = rows + EDGE
    low = me % 2 == 0

    turned = w_dt.T
    turned = jnp.concatenate([turned[0:8], turned[8:16]], axis=1)
    mix_dt = jnp.concatenate([w_bc.reshape(128, 256), turned], axis=0)
    far_x = hop(w_x, ZHOP, "far_x_rows")
    far_mix = hop(mix_dt, ZHOP, "far_mix_rows")
    edge = lax.ppermute(tokens[rows - EDGE :], "ctx", [(i, i + 1) for i in range(count - 1)])

    def part_of(wide_part, mix_part, q):
        piece = [wide_part[:, 256 * q : 256 * q + 256], mix_part[32 * q : 32 * q + 32]]
        if q == 1:
            piece.append(mix_part[128:136])
        return jnp.concatenate(piece, axis=0)

    both_x = [jnp.stack([part_of(w_x, mix_dt, q), part_of(far_x, far_mix, q)]) for q in range(4)]
    x_early = gather_some(both_x, "value")
    x_late = gather_rest(x_early, "value")
    tok = jnp.concatenate([after(edge, *x_early), tokens], axis=0)
    far_z = hop(after(w_z, *x_early), ZHOP, "far_gate_rows")
    both_z = [
        jnp.stack([w_z[:, 256 * q : 256 * q + 256], far_z[:, 256 * q : 256 * q + 256]])
        for q in range(4)
    ]
    z_early = gather_some([after(both_z[q], x_late[max(q, 1)]) for q in range(4)], "gate")
    slots = [{m: s for s, m in enumerate(masks(q, (0, 1)))} for q in range(4)]

    cumul, cum_r, end_c, grow, logs = call(
        step_kernel,
        (
            jax.ShapeDtypeStruct((rows, heads), f32),
            jax.ShapeDtypeStruct((heads, rows), f32),
            jax.ShapeDtypeStruct((rows, heads), f32),
            jax.ShapeDtypeStruct((rows, heads), f32),
            jax.ShapeDtypeStruct((2, 1024), f32),
        ),
        6,
        name="steps",
    )(idx, tokens, x_early[1][:, 160:168], x_late[1][:, 160:168], dt_bias[None], a_log[None])

    def early_kernel(idx_ref, tok_ref, *refs):
        for q in range(4):
            refs[4][:, 256 * q : 256 * q + 256] = side(
                tok_ref, idx_ref, refs[q], masks(q, (0, 1))[0:16]
            )

    def late_kernel(idx_ref, tok_ref, part_ref, *refs):
        early, late, out_ref = refs[0:4], refs[4:8], refs[8]
        for q in range(4):
            lanes = slice(256 * q, 256 * q + 256)
            part = side(tok_ref, idx_ref, late[q], masks(q, (0, 1))[16:32])
            out_ref[:, lanes] = (part + part_ref[:, lanes]).astype(bf16)
        part = mixed(tok_ref, idx_ref, early, late, slots)
        out_ref[:, 1024:1280] = part.astype(bf16)

    part = call(early_kernel, jax.ShapeDtypeStruct((wide, 1024), f32), 6, name="early_x")(
        idx, tok, *x_early
    )
    inner = call(late_kernel, jax.ShapeDtypeStruct((wide, 1280), bf16), 11, name="late_x")(
        idx, tok, part, *x_early, *x_late
    )

    skip = jnp.repeat(d_skip, 64)[None]
    x_c, bc, state, middle = call(
        state_kernel,
        (
            jax.ShapeDtypeStruct((rows, 1024), bf16),
            jax.ShapeDtypeStruct((rows, 256), bf16),
            jax.ShapeDtypeStruct((128, 1024), f32),
            jax.ShapeDtypeStruct((128, 1024), bf16),
        ),
        7,
        smem=0,
        name="state",
        scratch=(pltpu.VMEM((wide, 1024), f32), pltpu.VMEM((wide, 256), f32)),
    )(
        inner, conv_x, conv_bc.reshape(4, 256), bias_x[None], bias_bc.reshape(1, 256), end_c, logs,
    )
    def scan_block(b, x_rows):
        def kernel(*refs):
            scan_kernel(b, *refs)

        return call(
            kernel, jax.ShapeDtypeStruct((SPAN, 1024), f32), 6, smem=0, name=f"scan{b}"
        )(x_rows, bc, middle, cumul, cum_r, skip)

    my_log = logs[0]
    outs = []
    far_log = hop(logs, ZHOP, "far_log_rows")[0]
    whole = jnp.where(low, jnp.exp(far_log), 1.0)[None] * state
    whole_log = my_log + far_log
    before = jnp.zeros_like(whole)
    lead = jnp.zeros_like(whole_log)
    place = me // 2
    for mask, width in ((1, 1), (3, 2), (4, 4), (12, 8)):
        ready = whole
        message = hop(pack(whole, whole_log), mask * 2, f"state_rows_{mask}")
        if width >= 4:
            outs.append(scan_block(len(outs), after(x_c, whole)))
            message = after(message, outs[-1])
        got, got_log = unpack(message)
        earlier = (place ^ mask) // width < place // width
        before = before + jnp.where(earlier, jnp.exp(lead), 0.0)[None] * got
        whole = (
            jnp.where(earlier, 1.0, jnp.exp(got_log))[None] * whole
            + jnp.where(earlier, jnp.exp(whole_log), 1.0)[None] * got
        )
        lead = lead + jnp.where(earlier, got_log, 0.0)
        whole_log = whole_log + got_log
    keep = jnp.where(low, 1.0, jnp.exp(far_log))[None] * before
    send = jnp.where(low, jnp.exp(my_log)[None] * before + state, before).astype(bf16)
    carried = keep + hop(send, ZHOP, "far_state_rows").astype(f32)
    carried = carried.astype(bf16)

    z_late = gather_rest(
        [after(z_early[q], send if order(q)[3] == 24 else ready) for q in range(4)], "gate"
    )
    za = call(gate_kernel, jax.ShapeDtypeStruct((rows, 1024), f32), 6, name="gate")(
        idx, tokens, *z_early
    )
    gate = call(gate_late_kernel, jax.ShapeDtypeStruct((rows, 1024), f32), 7, name="gate_late")(
        idx, tokens, *z_late, za
    )
    return call(
        final_kernel, jax.ShapeDtypeStruct((rows, 1024), bf16), 7, smem=0, name="final"
    )(gate, *outs, bc, carried, grow, norm_gain[None])


def solution(mesh):
    placed = (
        P("ctx", None),
        P("ctx", "grp"),
        P("ctx", "grp"),
        P("ctx", "grp", None),
        P("ctx", "grp"),
        P(None, "grp"),
        P(None, "grp", None),
        P("grp"),
        P("grp", None),
        P("grp"),
        P("grp"),
        P("grp"),
        P("grp"),
    )
    return jax.shard_map(
        on_device, mesh=mesh, in_specs=placed, out_specs=P("ctx", "grp"), check_vma=False
    )
```

```python
import jax
import jax.numpy as jnp
from jax import lax
from jax.experimental import pallas as pl
from jax.experimental.pallas import tpu as pltpu
from jax.sharding import PartitionSpec as P

SPAN = 256
EDGE = 16
LIMIT = 12
HOPS = (8, 24, 2, 6)
ZHOP = 1


def swap(value, mask):
    count = lax.axis_size("ctx")
    return lax.ppermute(value, "ctx", [(i, i ^ mask) for i in range(count)])


def order(q):
    return [HOPS[(q + k) % 4] for k in range(4)]


def masks(q, zs):
    out = []
    for s in range(16):
        m = 0
        for k in range(4):
            if s >> k & 1:
                m ^= order(q)[k]
        out.extend(m ^ z for z in zs)
    return out


def hop(value, mask, scope):
    with jax.named_scope(scope):
        return swap(value, mask)


def gather_some(pieces, scope):
    now = list(pieces)
    for k in range(3):
        got = [hop(now[q], order(q)[k], f"{scope}_hop{k}_part{q}") for q in range(4)]
        now = [jnp.concatenate([now[q], got[q]], axis=0) for q in range(4)]
    return now


def gather_rest(now, scope):
    return [hop(now[q], order(q)[3], f"{scope}_hop3_part{q}") for q in range(4)]


def after(value, *others):
    return lax.optimization_barrier((value,) + others)[0]


def columns_of(tok_ref, idx_ref, wanted):
    return jnp.concatenate(
        [tok_ref[:, pl.ds(pl.multiple_of(idx_ref[m] * 128, 128), 128)] for m in wanted], axis=1
    )


def side(tok_ref, idx_ref, w, wanted):
    count = len(wanted)
    lhs = columns_of(tok_ref, idx_ref, wanted)
    rhs = w[:, 0:128, :].reshape(count * 128, w.shape[2])
    return jnp.dot(lhs, rhs, preferred_element_type=jnp.float32)


def mixed(tok_ref, idx_ref, early, late, slots):
    ms = sorted(slots[0])
    lhs = columns_of(tok_ref, idx_ref, ms)
    parts = []
    for m in ms:
        for q in range(4):
            s = slots[q][m]
            w = early[q] if s < 16 else late[q]
            parts.append(w[s % 16, 128:160, :])
    rhs = jnp.concatenate(parts, axis=0)
    return jnp.dot(lhs, rhs, preferred_element_type=jnp.float32)


VM = pl.BlockSpec(memory_space=pltpu.VMEM)
SM = pl.BlockSpec(memory_space=pltpu.SMEM)


def call(kernel, shapes, n_in, smem=1, limit=LIMIT, name=None, scratch=(), cost=None):
    return pl.pallas_call(
        kernel,
        out_shape=shapes,
        in_specs=[SM] * smem + [VM] * (n_in - smem),
        out_specs=jax.tree.map(lambda _: VM, shapes),
        scratch_shapes=scratch,
        cost_estimate=cost and pl.CostEstimate(flops=cost, transcendentals=0, bytes_accessed=0),
        compiler_params=pltpu.CompilerParams(vmem_limit_bytes=limit << 20),
        name=name,
    )


def state_kernel(p_ref, taps_x, taps_b, bias_x, bias_b, end_c, logs, x_ref, bc_ref, s_ref, mid_ref, xs, bs):
    xs[...] = p_ref[:, 0:1024].astype(jnp.float32)
    bs[...] = p_ref[:, 1024:1280].astype(jnp.float32)
    for b in range(2):
        base = EDGE + b * SPAN - 3

        def conv(ref, taps, bias):
            run = jnp.broadcast_to(bias[...], (SPAN, ref.shape[1]))
            for tap in range(4):
                run = run + taps[tap : tap + 1, :] * ref[base + tap : base + tap + SPAN, :]
            return run / (1.0 + jnp.exp(-run))

        x_c = conv(xs, taps_x, bias_x).astype(jnp.bfloat16)
        bc = conv(bs, taps_b, bias_b).astype(jnp.bfloat16)
        rows = slice(b * SPAN, b * SPAN + SPAN)
        x_ref[rows, :] = x_c
        bc_ref[rows, :] = bc
        x_f = x_c.astype(jnp.float32)
        scaled = []
        for h in range(end_c.shape[1]):
            lanes = slice(64 * h, 64 * h + 64)
            scaled.append((end_c[rows, h : h + 1] * x_f[:, lanes]).astype(jnp.bfloat16))
        xw = jnp.concatenate(scaled, axis=1)
        state = lax.dot_general(
            bc[:, 0:128], xw, (((0,), (0,)), ((), ())), preferred_element_type=jnp.float32
        )
        if b == 0:
            s_ref[...] = state
            mid_ref[...] = state.astype(jnp.bfloat16)
        else:
            s_ref[...] = jnp.exp(logs[1:2, :]) * s_ref[...] + state


def scan_kernel(b, x_ref, bc_ref, mid_ref, cum_c, cum_r, skip, y_ref):
    ii = lax.broadcasted_iota(jnp.int32, (SPAN, SPAN), 0)
    jj = lax.broadcasted_iota(jnp.int32, (SPAN, SPAN), 1)
    mask = ii >= jj
    rows = slice(b * SPAN, b * SPAN + SPAN)
    b_in, c_in = bc_ref[rows, 0:128], bc_ref[rows, 128:256]
    scores = lax.dot_general(
        c_in, b_in, (((1,), (1,)), ((), ())), preferred_element_type=jnp.float32
    )
    before = None
    if b == 1:
        before = jnp.dot(c_in, mid_ref[...], preferred_element_type=jnp.float32)
    for h in range(cum_c.shape[1]):
        lanes = slice(64 * h, 64 * h + 64)
        col = cum_c[rows, h : h + 1]
        gap = jnp.where(mask, col - cum_r[h : h + 1, rows], -1e30)
        weight = (jnp.exp(gap) * scores).astype(jnp.bfloat16)
        x_h = x_ref[rows, lanes]
        y = jnp.dot(weight, x_h, preferred_element_type=jnp.float32)
        y = y + skip[0:1, lanes] * x_h.astype(jnp.float32)
        if b == 1:
            y = y + jnp.exp(col) * before[:, lanes]
        y_ref[:, lanes] = y


def step_kernel(idx_ref, tok_ref, near, far, bias, a_log, cum_c, cum_r, end_c, grow, logs):
    rows, heads = cum_c.shape
    raw = jnp.zeros((rows, heads), jnp.float32)
    order_of = masks(1, (0, 1))
    for half, ref in enumerate((near, far)):
        lhs = columns_of(tok_ref, idx_ref, order_of[16 * half : 16 * half + 16])
        parts = []
        for s in range(16):
            w = ref[s].astype(jnp.float32)
            parts.append(jnp.concatenate([w[:, 0:128], w[:, 128:256]], axis=0))
        rhs = jnp.concatenate(parts, axis=1).astype(jnp.bfloat16)
        raw = raw + lax.dot_general(
            lhs, rhs, (((1,), (1,)), ((), ())), preferred_element_type=jnp.float32
        )
    raw = raw + bias[...]
    step = jnp.maximum(raw, 0.0) + jnp.log1p(jnp.exp(-jnp.abs(raw)))
    rate = -jnp.exp(a_log[...]) * step
    ii = lax.broadcasted_iota(jnp.int32, (SPAN, SPAN), 0)
    jj = lax.broadcasted_iota(jnp.int32, (SPAN, SPAN), 1)
    tri = jnp.where(ii >= jj, 1.0, 0.0)
    start = jnp.zeros((1, heads), jnp.float32)
    for b in range(rows // SPAN):
        span = slice(b * SPAN, b * SPAN + SPAN)
        cum = jnp.dot(
            tri, rate[span], preferred_element_type=jnp.float32, precision=lax.Precision.HIGHEST
        )
        last = cum[SPAN - 1 : SPAN, :]
        cum_c[span, :] = cum
        end_c[span, :] = jnp.exp(last - cum) * step[span]
        grow[span, :] = jnp.exp(cum + start)
        start = start + last
        side_by = cum - jnp.log(step[span])
        wide = jnp.concatenate([side_by, jnp.zeros((SPAN, 128 - heads), jnp.float32)], axis=1)
        cum_r[:, span] = wide.T[0:heads, :]
    for h in range(heads):
        lanes = slice(64 * h, 64 * h + 64)
        logs[0:1, lanes] = jnp.broadcast_to(start[:, h : h + 1], (1, 64))
        logs[1:2, lanes] = jnp.broadcast_to(last[:, h : h + 1], (1, 64))


def gate_kernel(idx_ref, tok_ref, *refs):
    for q in range(4):
        lanes = slice(256 * q, 256 * q + 256)
        refs[4][:, lanes] = side(tok_ref, idx_ref, refs[q], masks(q, (0, 1))[0:16])


def silu_of(tok_ref, idx_ref, w, za, q):
    g = za[:, 256 * q : 256 * q + 256] + side(tok_ref, idx_ref, w, masks(q, (0, 1))[16:32])
    g = g.astype(jnp.bfloat16).astype(jnp.float32)
    return g / (1.0 + jnp.exp(-g))


def gate_late_kernel(idx_ref, tok_ref, w0, w1, w3, za, out_ref):
    for i, (q, w) in enumerate(((0, w0), (1, w1), (3, w3))):
        out_ref[:, 256 * i : 256 * i + 256] = silu_of(tok_ref, idx_ref, w, za, q)


def final_kernel(idx_ref, tok_ref, w2, za, gates, y0, y1, c_ref, s_ref, grow, gain, out_ref):
    gate_2 = silu_of(tok_ref, idx_ref, w2, za, 2)
    inter = jnp.dot(c_ref[:, 128:256], s_ref[...], preferred_element_type=jnp.float32)
    heads = grow.shape[1]
    total = jnp.zeros((out_ref.shape[0], 1), jnp.float32)
    kept = []
    for h in range(heads // 2):
        lanes = slice(128 * h, 128 * h + 128)
        low = jnp.broadcast_to(grow[:, 2 * h : 2 * h + 1], (out_ref.shape[0], 128))
        high = jnp.broadcast_to(grow[:, 2 * h + 1 : 2 * h + 2], (out_ref.shape[0], 128))
        lane = lax.broadcasted_iota(jnp.int32, (1, 128), 1)
        y = jnp.concatenate([y0[:, lanes], y1[:, lanes]], axis=0)
        v = y + jnp.where(lane < 64, low, high) * inter[:, lanes]
        if h // 2 == 2:
            v = v * gate_2[:, 128 * (h % 2) : 128 * (h % 2) + 128]
        else:
            at = 128 * h if h < 4 else 128 * h - 256
            v = v * gates[:, at : at + 128]
        total = total + jnp.sum(v * v, axis=1, keepdims=True)
        kept.append(v)
    scale = lax.rsqrt(total / out_ref.shape[1] + 1e-05)
    for h in range(heads // 2):
        lanes = slice(128 * h, 128 * h + 128)
        out_ref[:, lanes] = (kept[h] * scale * gain[0:1, lanes]).astype(jnp.bfloat16)


def split(value):
    high = lax.reduce_precision(value, 8, 7)
    return high.astype(jnp.bfloat16), (value - high).astype(jnp.bfloat16)


def pack(state, log):
    high, low = split(log)
    tail = jnp.zeros((6,) + log.shape, jnp.bfloat16)
    return jnp.concatenate([state.astype(jnp.bfloat16), high[None], low[None], tail], axis=0)


def unpack(message):
    message = message.astype(jnp.float32)
    return message[0:128], message[128] + message[129]


def on_device(
    tokens, w_z, w_x, w_bc, w_dt, conv_x, conv_bc, bias_x, bias_bc, dt_bias, a_log, d_skip, norm_gain
):
    f32, bf16 = jnp.float32, jnp.bfloat16
    rows = tokens.shape[0]
    heads = w_dt.shape[1]
    me = lax.axis_index("ctx")
    count = lax.axis_size("ctx")
    idx = me.astype(jnp.int32) ^ jnp.arange(count, dtype=jnp.int32)
    wide = rows + EDGE
    low = me % 2 == 0

    turned = w_dt.T
    turned = jnp.concatenate([turned[0:8], turned[8:16]], axis=1)
    mix_dt = jnp.concatenate([w_bc.reshape(128, 256), turned], axis=0)
    far_x = hop(w_x, ZHOP, "far_x_rows")
    far_mix = hop(mix_dt, ZHOP, "far_mix_rows")
    edge = lax.ppermute(tokens[rows - EDGE :], "ctx", [(i, i + 1) for i in range(count - 1)])

    def part_of(wide_part, mix_part, q):
        piece = [wide_part[:, 256 * q : 256 * q + 256], mix_part[32 * q : 32 * q + 32]]
        if q == 1:
            piece.append(mix_part[128:136])
        return jnp.concatenate(piece, axis=0)

    both_x = [jnp.stack([part_of(w_x, mix_dt, q), part_of(far_x, far_mix, q)]) for q in range(4)]
    x_early = gather_some(both_x, "value")
    x_late = gather_rest(x_early, "value")
    tok = jnp.concatenate([after(edge, *x_early), tokens], axis=0)
    far_z = hop(after(w_z, *x_early), ZHOP, "far_gate_rows")
    both_z = [
        jnp.stack([w_z[:, 256 * q : 256 * q + 256], far_z[:, 256 * q : 256 * q + 256]])
        for q in range(4)
    ]
    z_early = gather_some([after(both_z[q], x_late[max(q, 1)]) for q in range(4)], "gate")
    slots = [{m: s for s, m in enumerate(masks(q, (0, 1)))} for q in range(4)]

    cumul, cum_r, end_c, grow, logs = call(
        step_kernel,
        (
            jax.ShapeDtypeStruct((rows, heads), f32),
            jax.ShapeDtypeStruct((heads, rows), f32),
            jax.ShapeDtypeStruct((rows, heads), f32),
            jax.ShapeDtypeStruct((rows, heads), f32),
            jax.ShapeDtypeStruct((2, 1024), f32),
        ),
        6,
        name="steps",
    )(idx, tokens, x_early[1][:, 160:168], x_late[1][:, 160:168], dt_bias[None], a_log[None])

    def early_kernel(idx_ref, tok_ref, *refs):
        for q in range(4):
            refs[4][:, 256 * q : 256 * q + 256] = side(
                tok_ref, idx_ref, refs[q], masks(q, (0, 1))[0:16]
            )

    def late_kernel(idx_ref, tok_ref, part_ref, *refs):
        early, late, out_ref = refs[0:4], refs[4:8], refs[8]
        for q in range(4):
            lanes = slice(256 * q, 256 * q + 256)
            part = side(tok_ref, idx_ref, late[q], masks(q, (0, 1))[16:32])
            out_ref[:, lanes] = (part + part_ref[:, lanes]).astype(bf16)
        part = mixed(tok_ref, idx_ref, early, late, slots)
        out_ref[:, 1024:1280] = part.astype(bf16)

    part = call(early_kernel, jax.ShapeDtypeStruct((wide, 1024), f32), 6, name="early_x")(
        idx, tok, *x_early
    )
    inner = call(late_kernel, jax.ShapeDtypeStruct((wide, 1280), bf16), 11, name="late_x")(
        idx, tok, part, *x_early, *x_late
    )

    skip = jnp.repeat(d_skip, 64)[None]
    x_c, bc, state, middle = call(
        state_kernel,
        (
            jax.ShapeDtypeStruct((rows, 1024), bf16),
            jax.ShapeDtypeStruct((rows, 256), bf16),
            jax.ShapeDtypeStruct((128, 1024), f32),
            jax.ShapeDtypeStruct((128, 1024), bf16),
        ),
        7,
        smem=0,
        name="state",
        scratch=(pltpu.VMEM((wide, 1024), f32), pltpu.VMEM((wide, 256), f32)),
    )(
        inner, conv_x, conv_bc.reshape(4, 256), bias_x[None], bias_bc.reshape(1, 256), end_c, logs,
    )
    def scan_block(b, x_rows):
        def kernel(*refs):
            scan_kernel(b, *refs)

        return call(
            kernel, jax.ShapeDtypeStruct((SPAN, 1024), f32), 6, smem=0, name=f"scan{b}"
        )(x_rows, bc, middle, cumul, cum_r, skip)

    my_log = logs[0]
    outs = []
    far_log = hop(logs, ZHOP, "far_log_rows")[0]
    whole = jnp.where(low, jnp.exp(far_log), 1.0)[None] * state
    whole_log = my_log + far_log
    before = jnp.zeros_like(whole)
    lead = jnp.zeros_like(whole_log)
    place = me // 2
    for mask, width in ((1, 1), (3, 2), (4, 4), (12, 8)):
        ready = whole
        message = hop(pack(whole, whole_log), mask * 2, f"state_rows_{mask}")
        if width >= 4:
            outs.append(scan_block(len(outs), after(x_c, whole)))
            message = after(message, outs[-1])
        got, got_log = unpack(message)
        earlier = (place ^ mask) // width < place // width
        before = before + jnp.where(earlier, jnp.exp(lead), 0.0)[None] * got
        whole = (
            jnp.where(earlier, 1.0, jnp.exp(got_log))[None] * whole
            + jnp.where(earlier, jnp.exp(whole_log), 1.0)[None] * got
        )
        lead = lead + jnp.where(earlier, got_log, 0.0)
        whole_log = whole_log + got_log
    keep = jnp.where(low, 1.0, jnp.exp(far_log))[None] * before
    send = jnp.where(low, jnp.exp(my_log)[None] * before + state, before).astype(bf16)
    carried = keep + hop(send, ZHOP, "far_state_rows").astype(f32)
    carried = carried.astype(bf16)

    z_late = gather_rest(
        [after(z_early[q], send if order(q)[3] == 24 else ready) for q in range(4)], "gate"
    )
    za = call(gate_kernel, jax.ShapeDtypeStruct((rows, 1024), f32), 6, name="gate")(
        idx, tokens, *z_early
    )
    gates = call(gate_late_kernel, jax.ShapeDtypeStruct((rows, 768), f32), 6, name="gate_late")(
        idx, tokens, z_late[0], z_late[1], z_late[3], za
    )
    return call(final_kernel, jax.ShapeDtypeStruct((rows, 1024), bf16), 11, name="final")(
        idx, tokens, z_late[2], za, gates, *outs, bc, carried, grow, norm_gain[None]
    )


def solution(mesh):
    placed = (
        P("ctx", None),
        P("ctx", "grp"),
        P("ctx", "grp"),
        P("ctx", "grp", None),
        P("ctx", "grp"),
        P(None, "grp"),
        P(None, "grp", None),
        P("grp"),
        P("grp", None),
        P("grp"),
        P("grp"),
        P("grp"),
        P("grp"),
    )
    return jax.shard_map(
        on_device, mesh=mesh, in_specs=placed, out_specs=P("ctx", "grp"), check_vma=False
    )
```

```python
import jax
import jax.numpy as jnp
from jax import lax
from jax.experimental import pallas as pl
from jax.experimental.pallas import tpu as pltpu
from jax.sharding import PartitionSpec as P

SPAN = 256
EDGE = 16
LIMIT = 12
HOPS = (8, 24, 2, 6)
ZHOP = 1


def swap(value, mask):
    count = lax.axis_size("ctx")
    return lax.ppermute(value, "ctx", [(i, i ^ mask) for i in range(count)])


def order(q):
    return [HOPS[(q + k) % 4] for k in range(4)]


def masks(q, zs):
    out = []
    for s in range(16):
        m = 0
        for k in range(4):
            if s >> k & 1:
                m ^= order(q)[k]
        out.extend(m ^ z for z in zs)
    return out


def hop(value, mask, scope):
    with jax.named_scope(scope):
        return swap(value, mask)


def gather_some(pieces, scope):
    now = list(pieces)
    for k in range(3):
        got = [hop(now[q], order(q)[k], f"{scope}_hop{k}_part{q}") for q in range(4)]
        now = [jnp.concatenate([now[q], got[q]], axis=0) for q in range(4)]
    return now


def gather_rest(now, scope):
    return [hop(now[q], order(q)[3], f"{scope}_hop3_part{q}") for q in range(4)]


def after(value, *others):
    return lax.optimization_barrier((value,) + others)[0]


def columns_of(tok_ref, idx_ref, wanted):
    return jnp.concatenate(
        [tok_ref[:, pl.ds(pl.multiple_of(idx_ref[m] * 128, 128), 128)] for m in wanted], axis=1
    )


def side(tok_ref, idx_ref, w, wanted):
    count = len(wanted)
    lhs = columns_of(tok_ref, idx_ref, wanted)
    rhs = w[:, 0:128, :].reshape(count * 128, w.shape[2])
    return jnp.dot(lhs, rhs, preferred_element_type=jnp.float32)


def mixed(tok_ref, idx_ref, early, late, slots):
    ms = sorted(slots[0])
    lhs = columns_of(tok_ref, idx_ref, ms)
    parts = []
    for m in ms:
        for q in range(4):
            s = slots[q][m]
            w = early[q] if s < 16 else late[q]
            parts.append(w[s % 16, 128:160, :])
    rhs = jnp.concatenate(parts, axis=0)
    return jnp.dot(lhs, rhs, preferred_element_type=jnp.float32)


VM = pl.BlockSpec(memory_space=pltpu.VMEM)
SM = pl.BlockSpec(memory_space=pltpu.SMEM)


def call(kernel, shapes, n_in, smem=1, limit=LIMIT, name=None, scratch=(), cost=None):
    return pl.pallas_call(
        kernel,
        out_shape=shapes,
        in_specs=[SM] * smem + [VM] * (n_in - smem),
        out_specs=jax.tree.map(lambda _: VM, shapes),
        scratch_shapes=scratch,
        cost_estimate=cost and pl.CostEstimate(flops=cost, transcendentals=0, bytes_accessed=0),
        compiler_params=pltpu.CompilerParams(vmem_limit_bytes=limit << 20),
        name=name,
    )


def state_kernel(p_ref, taps_x, taps_b, bias_x, bias_b, end_c, logs, x_ref, bc_ref, s_ref, mid_ref, xs, bs):
    xs[...] = p_ref[:, 0:1024].astype(jnp.float32)
    bs[...] = p_ref[:, 1024:1280].astype(jnp.float32)
    for b in range(2):
        base = EDGE + b * SPAN - 3

        def conv(ref, taps, bias):
            run = jnp.broadcast_to(bias[...], (SPAN, ref.shape[1]))
            for tap in range(4):
                run = run + taps[tap : tap + 1, :] * ref[base + tap : base + tap + SPAN, :]
            return run / (1.0 + jnp.exp(-run))

        x_c = conv(xs, taps_x, bias_x).astype(jnp.bfloat16)
        bc = conv(bs, taps_b, bias_b).astype(jnp.bfloat16)
        rows = slice(b * SPAN, b * SPAN + SPAN)
        x_ref[rows, :] = x_c
        bc_ref[rows, :] = bc
        x_f = x_c.astype(jnp.float32)
        scaled = []
        for h in range(end_c.shape[1]):
            lanes = slice(64 * h, 64 * h + 64)
            scaled.append((end_c[rows, h : h + 1] * x_f[:, lanes]).astype(jnp.bfloat16))
        xw = jnp.concatenate(scaled, axis=1)
        state = lax.dot_general(
            bc[:, 0:128], xw, (((0,), (0,)), ((), ())), preferred_element_type=jnp.float32
        )
        if b == 0:
            s_ref[...] = state
            mid_ref[...] = state.astype(jnp.bfloat16)
        else:
            s_ref[...] = jnp.exp(logs[1:2, :]) * s_ref[...] + state


def scan_kernel(b, x_ref, bc_ref, mid_ref, cum_c, cum_r, skip, y_ref):
    ii = lax.broadcasted_iota(jnp.int32, (SPAN, SPAN), 0)
    jj = lax.broadcasted_iota(jnp.int32, (SPAN, SPAN), 1)
    mask = ii >= jj
    rows = slice(b * SPAN, b * SPAN + SPAN)
    b_in, c_in = bc_ref[rows, 0:128], bc_ref[rows, 128:256]
    scores = lax.dot_general(
        c_in, b_in, (((1,), (1,)), ((), ())), preferred_element_type=jnp.float32
    )
    before = None
    if b == 1:
        before = jnp.dot(c_in, mid_ref[...], preferred_element_type=jnp.float32)
    for h in range(cum_c.shape[1]):
        lanes = slice(64 * h, 64 * h + 64)
        col = cum_c[rows, h : h + 1]
        gap = jnp.where(mask, col - cum_r[h : h + 1, rows], -1e30)
        weight = (jnp.exp(gap) * scores).astype(jnp.bfloat16)
        x_h = x_ref[rows, lanes]
        y = jnp.dot(weight, x_h, preferred_element_type=jnp.float32)
        y = y + skip[0:1, lanes] * x_h.astype(jnp.float32)
        if b == 1:
            y = y + jnp.exp(col) * before[:, lanes]
        y_ref[:, lanes] = y


def step_kernel(idx_ref, tok_ref, near, far, bias, a_log, cum_c, cum_r, end_c, grow, logs):
    rows, heads = cum_c.shape
    raw = jnp.zeros((rows, heads), jnp.float32)
    order_of = masks(1, (0, 1))
    for half, ref in enumerate((near, far)):
        lhs = columns_of(tok_ref, idx_ref, order_of[16 * half : 16 * half + 16])
        parts = []
        for s in range(16):
            w = ref[s].astype(jnp.float32)
            parts.append(jnp.concatenate([w[:, 0:128], w[:, 128:256]], axis=0))
        rhs = jnp.concatenate(parts, axis=1).astype(jnp.bfloat16)
        raw = raw + lax.dot_general(
            lhs, rhs, (((1,), (1,)), ((), ())), preferred_element_type=jnp.float32
        )
    raw = raw + bias[...]
    step = jnp.maximum(raw, 0.0) + jnp.log1p(jnp.exp(-jnp.abs(raw)))
    rate = -jnp.exp(a_log[...]) * step
    ii = lax.broadcasted_iota(jnp.int32, (SPAN, SPAN), 0)
    jj = lax.broadcasted_iota(jnp.int32, (SPAN, SPAN), 1)
    tri = jnp.where(ii >= jj, 1.0, 0.0)
    start = jnp.zeros((1, heads), jnp.float32)
    for b in range(rows // SPAN):
        span = slice(b * SPAN, b * SPAN + SPAN)
        cum = jnp.dot(
            tri, rate[span], preferred_element_type=jnp.float32, precision=lax.Precision.HIGHEST
        )
        last = cum[SPAN - 1 : SPAN, :]
        cum_c[span, :] = cum
        end_c[span, :] = jnp.exp(last - cum) * step[span]
        grow[span, :] = jnp.exp(cum + start)
        start = start + last
        side_by = cum - jnp.log(step[span])
        wide = jnp.concatenate([side_by, jnp.zeros((SPAN, 128 - heads), jnp.float32)], axis=1)
        cum_r[:, span] = wide.T[0:heads, :]
    for h in range(heads):
        lanes = slice(64 * h, 64 * h + 64)
        logs[0:1, lanes] = jnp.broadcast_to(start[:, h : h + 1], (1, 64))
        logs[1:2, lanes] = jnp.broadcast_to(last[:, h : h + 1], (1, 64))


def gate_kernel(idx_ref, tok_ref, *refs):
    for q in range(4):
        lanes = slice(256 * q, 256 * q + 256)
        refs[4][:, lanes] = side(tok_ref, idx_ref, refs[q], masks(q, (0, 1))[0:16])


def silu_of(tok_ref, idx_ref, w, za, q):
    g = za[:, 256 * q : 256 * q + 256] + side(tok_ref, idx_ref, w, masks(q, (0, 1))[16:32])
    g = g.astype(jnp.bfloat16).astype(jnp.float32)
    return g / (1.0 + jnp.exp(-g))


def gate_late_kernel(idx_ref, tok_ref, w0, w1, w3, za, out_ref):
    for i, (q, w) in enumerate(((0, w0), (1, w1), (3, w3))):
        out_ref[:, 256 * i : 256 * i + 256] = silu_of(tok_ref, idx_ref, w, za, q)


def final_kernel(idx_ref, tok_ref, w2, za, gates, y0, y1, c_ref, s_ref, grow, gain, out_ref):
    gate_2 = silu_of(tok_ref, idx_ref, w2, za, 2)
    inter = jnp.dot(c_ref[:, 128:256], s_ref[...], preferred_element_type=jnp.float32)
    heads = grow.shape[1]
    total = jnp.zeros((out_ref.shape[0], 1), jnp.float32)
    kept = []
    for h in range(heads // 2):
        lanes = slice(128 * h, 128 * h + 128)
        low = jnp.broadcast_to(grow[:, 2 * h : 2 * h + 1], (out_ref.shape[0], 128))
        high = jnp.broadcast_to(grow[:, 2 * h + 1 : 2 * h + 2], (out_ref.shape[0], 128))
        lane = lax.broadcasted_iota(jnp.int32, (1, 128), 1)
        y = jnp.concatenate([y0[:, lanes], y1[:, lanes]], axis=0)
        v = y + jnp.where(lane < 64, low, high) * inter[:, lanes]
        if h // 2 == 2:
            v = v * gate_2[:, 128 * (h % 2) : 128 * (h % 2) + 128]
        else:
            at = 128 * h if h < 4 else 128 * h - 256
            v = v * gates[:, at : at + 128]
        total = total + jnp.sum(v * v, axis=1, keepdims=True)
        kept.append(v)
    scale = lax.rsqrt(total / out_ref.shape[1] + 1e-05)
    for h in range(heads // 2):
        lanes = slice(128 * h, 128 * h + 128)
        out_ref[:, lanes] = (kept[h] * scale * gain[0:1, lanes]).astype(jnp.bfloat16)


def split(value):
    high = lax.reduce_precision(value, 8, 7)
    return high.astype(jnp.bfloat16), (value - high).astype(jnp.bfloat16)


def pack(state, log):
    high, low = split(log)
    tail = jnp.zeros((6,) + log.shape, jnp.bfloat16)
    return jnp.concatenate([state.astype(jnp.bfloat16), high[None], low[None], tail], axis=0)


def unpack(message):
    message = message.astype(jnp.float32)
    return message[0:128], message[128] + message[129]


def on_device(
    tokens, w_z, w_x, w_bc, w_dt, conv_x, conv_bc, bias_x, bias_bc, dt_bias, a_log, d_skip, norm_gain
):
    f32, bf16 = jnp.float32, jnp.bfloat16
    rows = tokens.shape[0]
    heads = w_dt.shape[1]
    me = lax.axis_index("ctx")
    count = lax.axis_size("ctx")
    idx = me.astype(jnp.int32) ^ jnp.arange(count, dtype=jnp.int32)
    wide = rows + EDGE
    low = me % 2 == 0

    turned = w_dt.T
    turned = jnp.concatenate([turned[0:8], turned[8:16]], axis=1)
    mix_dt = jnp.concatenate([w_bc.reshape(128, 256), turned], axis=0)
    far_x = hop(w_x, ZHOP, "far_x_rows")
    own_first = [w_x[:, 256 * q : 256 * q + 256] for q in range(4)]
    far_mix = hop(after(mix_dt, *own_first), ZHOP, "far_mix_rows")
    edge = lax.ppermute(tokens[rows - EDGE :], "ctx", [(i, i + 1) for i in range(count - 1)])

    def part_of(wide_part, mix_part, q):
        piece = [wide_part[:, 256 * q : 256 * q + 256], mix_part[32 * q : 32 * q + 32]]
        if q == 1:
            piece.append(mix_part[128:136])
        return jnp.concatenate(piece, axis=0)

    both_x = [jnp.stack([part_of(w_x, mix_dt, q), part_of(far_x, far_mix, q)]) for q in range(4)]
    x_early = gather_some(both_x, "value")
    x_late = gather_rest(x_early, "value")
    tok = jnp.concatenate([after(edge, *x_early), tokens], axis=0)
    far_z = hop(after(w_z, *x_early), ZHOP, "far_gate_rows")
    both_z = [
        jnp.stack([w_z[:, 256 * q : 256 * q + 256], far_z[:, 256 * q : 256 * q + 256]])
        for q in range(4)
    ]
    z_early = gather_some([after(both_z[q], x_late[max(q, 1)]) for q in range(4)], "gate")
    slots = [{m: s for s, m in enumerate(masks(q, (0, 1)))} for q in range(4)]

    cumul, cum_r, end_c, grow, logs = call(
        step_kernel,
        (
            jax.ShapeDtypeStruct((rows, heads), f32),
            jax.ShapeDtypeStruct((heads, rows), f32),
            jax.ShapeDtypeStruct((rows, heads), f32),
            jax.ShapeDtypeStruct((rows, heads), f32),
            jax.ShapeDtypeStruct((2, 1024), f32),
        ),
        6,
        name="steps",
    )(idx, tokens, x_early[1][:, 160:168], x_late[1][:, 160:168], dt_bias[None], a_log[None])

    def early_kernel(idx_ref, tok_ref, *refs):
        for q in range(4):
            refs[4][:, 256 * q : 256 * q + 256] = side(
                tok_ref, idx_ref, refs[q], masks(q, (0, 1))[0:16]
            )

    def late_kernel(idx_ref, tok_ref, part_ref, *refs):
        early, late, out_ref = refs[0:4], refs[4:8], refs[8]
        for q in range(4):
            lanes = slice(256 * q, 256 * q + 256)
            part = side(tok_ref, idx_ref, late[q], masks(q, (0, 1))[16:32])
            out_ref[:, lanes] = (part + part_ref[:, lanes]).astype(bf16)
        part = mixed(tok_ref, idx_ref, early, late, slots)
        out_ref[:, 1024:1280] = part.astype(bf16)

    part = call(early_kernel, jax.ShapeDtypeStruct((wide, 1024), f32), 6, name="early_x")(
        idx, tok, *x_early
    )
    inner = call(late_kernel, jax.ShapeDtypeStruct((wide, 1280), bf16), 11, name="late_x")(
        idx, tok, part, *x_early, *x_late
    )

    skip = jnp.repeat(d_skip, 64)[None]
    x_c, bc, state, middle = call(
        state_kernel,
        (
            jax.ShapeDtypeStruct((rows, 1024), bf16),
            jax.ShapeDtypeStruct((rows, 256), bf16),
            jax.ShapeDtypeStruct((128, 1024), f32),
            jax.ShapeDtypeStruct((128, 1024), bf16),
        ),
        7,
        smem=0,
        name="state",
        scratch=(pltpu.VMEM((wide, 1024), f32), pltpu.VMEM((wide, 256), f32)),
    )(
        inner, conv_x, conv_bc.reshape(4, 256), bias_x[None], bias_bc.reshape(1, 256), end_c, logs,
    )
    def scan_block(b, x_rows):
        def kernel(*refs):
            scan_kernel(b, *refs)

        return call(
            kernel, jax.ShapeDtypeStruct((SPAN, 1024), f32), 6, smem=0, name=f"scan{b}"
        )(x_rows, bc, middle, cumul, cum_r, skip)

    my_log = logs[0]
    outs = []
    far_log = hop(logs, ZHOP, "far_log_rows")[0]
    whole = jnp.where(low, jnp.exp(far_log), 1.0)[None] * state
    whole_log = my_log + far_log
    before = jnp.zeros_like(whole)
    lead = jnp.zeros_like(whole_log)
    place = me // 2
    for mask, width in ((1, 1), (3, 2), (4, 4), (12, 8)):
        ready = whole
        message = hop(pack(whole, whole_log), mask * 2, f"state_rows_{mask}")
        if width >= 4:
            outs.append(scan_block(len(outs), after(x_c, whole)))
            message = after(message, outs[-1])
        got, got_log = unpack(message)
        earlier = (place ^ mask) // width < place // width
        before = before + jnp.where(earlier, jnp.exp(lead), 0.0)[None] * got
        whole = (
            jnp.where(earlier, 1.0, jnp.exp(got_log))[None] * whole
            + jnp.where(earlier, jnp.exp(whole_log), 1.0)[None] * got
        )
        lead = lead + jnp.where(earlier, got_log, 0.0)
        whole_log = whole_log + got_log
    keep = jnp.where(low, 1.0, jnp.exp(far_log))[None] * before
    send = jnp.where(low, jnp.exp(my_log)[None] * before + state, before).astype(bf16)
    carried = keep + hop(send, ZHOP, "far_state_rows").astype(f32)
    carried = carried.astype(bf16)

    z_late = gather_rest(
        [after(z_early[q], send if order(q)[3] == 24 else ready) for q in range(4)], "gate"
    )
    za = call(gate_kernel, jax.ShapeDtypeStruct((rows, 1024), f32), 6, name="gate")(
        idx, tokens, *z_early
    )
    gates = call(gate_late_kernel, jax.ShapeDtypeStruct((rows, 768), f32), 6, name="gate_late")(
        idx, tokens, z_late[0], z_late[1], z_late[3], za
    )
    return call(final_kernel, jax.ShapeDtypeStruct((rows, 1024), bf16), 11, name="final")(
        idx, tokens, z_late[2], za, gates, *outs, bc, carried, grow, norm_gain[None]
    )


def solution(mesh):
    placed = (
        P("ctx", None),
        P("ctx", "grp"),
        P("ctx", "grp"),
        P("ctx", "grp", None),
        P("ctx", "grp"),
        P(None, "grp"),
        P(None, "grp", None),
        P("grp"),
        P("grp", None),
        P("grp"),
        P("grp"),
        P("grp"),
        P("grp"),
    )
    return jax.shard_map(
        on_device, mesh=mesh, in_specs=placed, out_specs=P("ctx", "grp"), check_vma=False
    )
```
